32 devices in a mesh: dom: 2 (over y), row: 4 (over x, core), col: 4 (over z).
Axes of the slice: x: 2, y: 2, z: 4, core: 2. Of those that a mesh axis runs over, the one named last changes fastest.
Arguments:
- ext_ext: float32 [4, 2304, 2304], P('dom', 'row', 'col'), parts along dimension 0, may hold values from -0.125 to 0.125
- ext_int: float32 [4, 2304, 768], P('dom', 'row', 'col'), parts along dimension 0, may hold values from -0.21875 to 0.21875
- int_ext: float32 [4, 768, 2304], P('dom', 'row', 'col'), parts along dimension 0, may hold values from -0.125 to 0.125
- int_int: float32 [4, 768, 768], P('dom', 'row', 'col'), parts along dimension 0, may hold values from -2 to 2, as said below
- boundary_data: float32 [4, 2304, 128], P('dom', 'row', 'col'), parts along dimension 0, may hold values from -6 to 6
- leaf_ext_ext: float32 [32, 2, 576, 576], P(('dom', 'row', 'col')), parts along dimension 0, may hold values from -0.25 to 0.25
- leaf_ext_int: float32 [32, 2, 576, 192], P(('dom', 'row', 'col')), parts along dimension 0, may hold values from -0.4375 to 0.4375
- leaf_int_ext: float32 [32, 2, 192, 576], P(('dom', 'row', 'col')), parts along dimension 0, may hold values from -0.25 to 0.25
- leaf_int_int: float32 [32, 2, 192, 192], P(('dom', 'row', 'col')), parts along dimension 0, may hold values from -2 to 2, as said below
Outputs:
- parent_map: float32 [4, 2, 2304, 2304], P('dom', None, 'row', 'col'), parts along dimension 0
- solve_op: float32 [4, 768, 2304], P('dom', 'row', 'col'), parts along dimension 0
- interface_values: float32 [1536, 128], P(('dom', 'row'), 'col'), parts along dimension 0
- leaf_parent: float32 [32, 2, 2, 576, 576], P(('dom', 'row', 'col')), parts along dimension 0
- leaf_solve: float32 [32, 2, 192, 576], P(('dom', 'row', 'col')), parts along dimension 0
The draws below stay inside these ranges and needn't reach their ends.
There are 2 independent parts, one for each index of `dom`. The reference program is written for one: setup_inputs(seed, part) draws one part's arguments, and reference() takes and returns one part's arrays. A program takes and returns all parts, laid end to end along the dimension named above; each array names one. Nothing has to cross between parts.
Inputs may be any that keep to these rules, and one draw needn't show every extreme that they name: `int_int`: off-diagonal entries are small against a diagonal between 1 and 2 in each child's map. `leaf_int_int`: off-diagonal entries are small against a diagonal between 1 and 2 in each child's map.
All inputs are finite; a program needn't handle non-finite values.
Results may differ from the reference program's by a relative error of at most 0.00022.
Values sent between devices are 32-bit elements; how exact they have to be, the bound alone decides.
No kernel may reach another device: no remote copies, remote signals or barrier semaphores. Data moves between devices by JAX's collectives and lax.ppermute only.
A program may use at most 128 MiB of HBM per device.

```python
import jax
import jax.numpy as jnp
from jax import lax

SIDE = 768
LEAF = 192
SOURCES = 128
ITERS = 2
BOXES = 16


def dominant(key, lead, size):
    first, second = jax.random.split(key)
    spread = 0.4 / size ** 0.5
    off_diag = jax.random.normal(first, lead + (size, size), jnp.float32) * spread
    diag_vals = jax.random.uniform(second, lead + (size,), jnp.float32, 1.0, 2.0)
    eye = jnp.eye(size, dtype=jnp.float32)
    return off_diag * (1.0 - eye) + diag_vals[..., :, None] * eye


def draw_int_int(key, part):
    return dominant(jax.random.fold_in(key, 17), (2,), SIDE)


def draw_leaf_int_int(key, part):
    return dominant(jax.random.fold_in(key, 29), (BOXES, 2), LEAF)


def block_levels(rng, extent, cuts, least, high):
    gain, own = 1.0, jax.random.fold_in(rng, 6)
    for axis_at, parts in cuts:
        draws = jnp.exp(jax.random.uniform(jax.random.fold_in(own, axis_at), (parts,), jnp.float32, least / len(cuts), high / len(cuts)))
        gain = gain * jnp.repeat(draws, extent[axis_at] // parts).reshape([-1 if axis == axis_at else 1 for axis in range(len(extent))])
    return gain


def scatter_about(key, extent, scale, limit, cuts=(), kind=jnp.bfloat16):
    level = block_levels(key, extent, cuts, -0.22, 0.18) if cuts else 1.0
    result = jax.random.normal(key, extent, jnp.float32) * scale * level
    return jnp.minimum(jnp.maximum(result, -limit), limit).astype(kind)


def setup_inputs(seed: int = 0, part: int = 0) -> dict:
    streams_of = jax.random.split(jax.random.key(seed), 10)
    part_keys = jax.random.split(jax.random.fold_in(streams_of[9], part), 10)
    ext_ext = scatter_about(part_keys[0], (2, 3 * SIDE, 3 * SIDE), (3 * SIDE) ** -0.5, 0.125, ((1, 4), (2, 4)), jnp.float32)
    ext_int = scatter_about(part_keys[1], (2, 3 * SIDE, SIDE), SIDE ** -0.5, 0.21875, ((1, 4), (2, 4)), jnp.float32)
    int_ext = scatter_about(part_keys[2], (2, SIDE, 3 * SIDE), (3 * SIDE) ** -0.5, 0.125, ((1, 4), (2, 4)), jnp.float32)
    int_int = draw_int_int(jax.random.fold_in(jax.random.fold_in(streams_of[9], part), 71), part)
    boundary_data = scatter_about(part_keys[4], (2, 3 * SIDE, SOURCES), 1.0, 6.0, ((1, 4), (2, 4)), jnp.float32)
    leaf_ext_ext = scatter_about(part_keys[5], (BOXES, 2, 3 * LEAF, 3 * LEAF), (3 * LEAF) ** -0.5, 0.25, ((0, 16),), jnp.float32)
    leaf_ext_int = scatter_about(part_keys[6], (BOXES, 2, 3 * LEAF, LEAF), LEAF ** -0.5, 0.4375, ((0, 16),), jnp.float32)
    leaf_int_ext = scatter_about(part_keys[7], (BOXES, 2, LEAF, 3 * LEAF), (3 * LEAF) ** -0.5, 0.25, ((0, 16),), jnp.float32)
    leaf_int_int = draw_leaf_int_int(jax.random.fold_in(jax.random.fold_in(streams_of[9], part), 71), part)
    return dict(ext_ext=ext_ext, ext_int=ext_int, int_ext=int_ext, int_int=int_int, boundary_data=boundary_data, leaf_ext_ext=leaf_ext_ext, leaf_ext_int=leaf_ext_int, leaf_int_ext=leaf_int_ext, leaf_int_int=leaf_int_int)


def matmul(a, b):
    return jnp.dot(a, b, precision=lax.Precision.HIGHEST, preferred_element_type=jnp.float32)


def newton(joint):
    size = joint.shape[0]
    eye = jnp.eye(size, dtype=jnp.float32)
    current = eye / jnp.diagonal(joint)[None, :]
    for step in range(ITERS):
        product = matmul(joint, current)
        current = 2.0 * current - matmul(current, product)
    return current


def merge_local(ee, ei, ie, ii):
    side = ii.shape[1]
    third = ee.shape[1]
    inverse = newton(ii[0] + ii[1])
    coupling = jnp.concatenate([ie[0], ie[1]], axis=1)
    solution = -matmul(inverse, coupling)
    solve = jnp.stack([solution[:, :third], solution[:, third:]])
    lifted = matmul(ei.reshape(2 * third, side), solution)
    lifted = lifted.reshape(2, third, 2, third).transpose(0, 2, 1, 3)
    pairs = jnp.eye(2, dtype=jnp.float32)
    parent = lifted + pairs[:, :, None, None] * ee[:, None]
    return parent, solve, solution


def leaf_merge(group):
    parent, solve, solution = merge_local(group[0], group[1], group[2], group[3])
    return parent, solve


def reference(ext_ext, ext_int, int_ext, int_int, boundary_data, leaf_ext_ext, leaf_ext_int, leaf_int_ext, leaf_int_int):
    parent_map, solve_op, solution = merge_local(ext_ext, ext_int, int_ext, int_int)
    interface_values = matmul(solution, boundary_data.reshape(6 * SIDE, SOURCES))
    leaf_parent, leaf_solve = lax.map(leaf_merge, (leaf_ext_ext, leaf_ext_int, leaf_int_ext, leaf_int_int))
    return parent_map, solve_op, interface_values, leaf_parent, leaf_solve
```

```python
import functools

import jax
import jax.numpy as jnp
from jax import lax
from jax.experimental import pallas as pl
from jax.experimental.pallas import tpu as pltpu
from jax.sharding import PartitionSpec as P

ITERS = 2
F32 = jnp.float32
BF16 = jnp.bfloat16
VMEM_LIMIT = 58 * 1024 * 1024


def pow2(n):
    return n & (n - 1) == 0


def owner(i, k, n):
    return i ^ k if pow2(n) else lax.rem(i + k, n)


def send(x, axis, k):
    n = lax.axis_size(axis)
    if pow2(n):
        return lax.ppermute(x, axis, [(i, i ^ k) for i in range(n)])
    return lax.ppermute(x, axis, [((i + k) % n, i) for i in range(n)])


def gather_slots(x, axis):
    n = lax.axis_size(axis)
    slots = {0: x}
    if pow2(n):
        bit = n // 2
        while bit:
            for k in sorted(slots):
                slots[k | bit] = send(slots[k], axis, bit)
            bit //= 2
    else:
        for k in range(1, n):
            slots[k] = send(x, axis, k)
    return [slots[k] for k in range(n)]


def in_order(slots, axis):
    n = lax.axis_size(axis)
    i = lax.axis_index(axis)
    if pow2(n):
        bit = 1
        while bit < n:
            flip = (i & bit) != 0
            slots = [jnp.where(flip, slots[k ^ bit], slots[k]) for k in range(n)]
            bit *= 2
        return slots
    stacked = jnp.stack(slots)
    return [lax.dynamic_index_in_dim(stacked, lax.rem(b - i + n, n), 0, False) for b in range(n)]


def split(x):
    head = x.astype(BF16)
    return head, (x - head.astype(F32)).astype(BF16)


def dot(a, b):
    return jnp.dot(a, b, preferred_element_type=F32)


def dot3(a, b):
    return dot(a[0], b[0]) + (dot(a[0], b[1]) + dot(a[1], b[0]))


def first_step(joint, eye):
    kept = jnp.where(eye, joint, 0.0)
    down = 1.0 / jnp.sum(kept, axis=1, keepdims=True)
    across = 1.0 / jnp.sum(kept, axis=0, keepdims=True)
    return down, across


def tile_of(rows, most):
    best = 8
    for t in range(16, min(rows, most) + 1, 16):
        if rows % t == 0:
            best = t
    return best


def leaf_kernel(ee, ei, ie, ii, parent, solve):
    joint = ii[0, 0] + ii[0, 1]
    side = joint.shape[0]
    eye = lax.broadcasted_iota(jnp.int32, joint.shape, 0) == lax.broadcasted_iota(jnp.int32, joint.shape, 1)
    down, across = first_step(joint, eye)
    current = jnp.where(eye, 2.0 * across, 0.0) - down * joint * across
    for step in range(ITERS - 1):
        pair = split(current)
        current = 2.0 * current - dot3(pair, split(dot3(split(joint), pair)))
    inverse = split(current)
    for b in range(2):
        sol = -dot3(inverse, split(ie[0, b]))
        solve[0, b] = sol
        sol = split(sol)
        for a in range(2):
            out = dot3(split(ei[0, a]), sol)
            parent[0, a, b] = out + ee[0, a] if a == b else out


def leaf_merge(ee, ei, ie, ii):
    boxes, _, ext, side = ei.shape
    third = ie.shape[3]
    box = lambda *s: pl.BlockSpec((1,) + s, lambda i: (i,) + (0,) * len(s))
    return pl.pallas_call(
        leaf_kernel,
        grid=(boxes,),
        in_specs=[box(2, ext, third), box(2, ext, side), box(2, side, third), box(2, side, side)],
        out_specs=[box(2, 2, ext, third), box(2, side, third)],
        out_shape=[
            jax.ShapeDtypeStruct((boxes, 2, 2, ext, third), F32),
            jax.ShapeDtypeStruct((boxes, 2, side, third), F32),
        ],
        compiler_params=pltpu.CompilerParams(vmem_limit_bytes=VMEM_LIMIT),
        cost_estimate=pl.CostEstimate(flops=boxes * 24 * ext * side * third, transcendentals=0, bytes_accessed=boxes * 4 * 6 * ext * third),
        name="leaf",
    )(ee, ei, ie, ii)


def solve_kernel(n_row, *refs):
    joints, couplings = refs[:n_row], refs[n_row : 2 * n_row]
    solve, head, tail = refs[2 * n_row : 2 * n_row + 3]
    joint, jh, jl, x1, xh, xl, mh, ml, cpl, ch, cl, full, sem = refs[2 * n_row + 3 :]
    me = lax.axis_index("row")
    side = joint.shape[0]
    rows = side // n_row
    tm = tile_of(side, 256)
    j_copies, c_copies = [], []
    for k in range(n_row):
        at = pl.ds(pl.multiple_of(owner(me, k, n_row) * rows, rows), rows)
        j_copies.append(pltpu.make_async_copy(joints[k], joint.at[at], sem.at[0, k]))
        for b in range(2):
            c_copies.append(pltpu.make_async_copy(couplings[k].at[b], cpl.at[b, at], sem.at[1 + b, k]))
    for copy in j_copies + c_copies:
        copy.start()
    for copy in j_copies:
        copy.wait()

    def tile(i):
        return pl.ds(pl.multiple_of(i * tm, tm), tm)

    def eye(i):
        shape = (tm, side)
        return lax.broadcasted_iota(jnp.int32, shape, 0) + i * tm == lax.broadcasted_iota(jnp.int32, shape, 1)

    def diag_part(i, acc):
        return acc + jnp.sum(jnp.where(eye(i), joint[tile(i)], 0.0), axis=0, keepdims=True)

    across = 1.0 / lax.fori_loop(0, side // tm, diag_part, jnp.zeros((1, side), F32))

    def prepare(i, _):
        j = joint[tile(i)]
        mask = eye(i)
        down = 1.0 / jnp.sum(jnp.where(mask, j, 0.0), axis=1, keepdims=True)
        jh[tile(i)], jl[tile(i)] = split(j)
        x = jnp.where(mask, 2.0 * across, 0.0) - down * j * across
        x1[tile(i)] = x
        xh[tile(i)], xl[tile(i)] = split(x)
        return 0

    lax.fori_loop(0, side // tm, prepare, 0)

    def middle(i, _):
        m = dot3((jh[tile(i)], jl[tile(i)]), (xh[...], xl[...]))
        mh[tile(i)], ml[tile(i)] = split(m)
        return 0

    lax.fori_loop(0, side // tm, middle, 0)
    for copy in c_copies:
        copy.wait()

    def halve(i, _):
        for b in range(2):
            ch[b, tile(i)], cl[b, tile(i)] = split(cpl[b, tile(i)])
        return 0

    lax.fori_loop(0, side // tm, halve, 0)

    def last(i, _):
        x2 = split(2.0 * x1[tile(i)] - dot3((xh[tile(i)], xl[tile(i)]), (mh[...], ml[...])))
        for b in range(2):
            s = -dot3(x2, (ch[b], cl[b]))
            full[b, tile(i)] = s
            head[b, tile(i)], tail[b, tile(i)] = split(s)
        return 0

    lax.fori_loop(0, side // tm, last, 0)
    mine = pl.ds(pl.multiple_of(me * rows, rows), rows)
    for b in range(2):
        solve[b] = full[b, mine]


def solve_columns(joints, couplings):
    n_row = len(joints)
    rows, side = joints[0].shape
    third = couplings[0].shape[2]
    any_ = pl.BlockSpec(memory_space=pl.ANY)
    vm = pl.BlockSpec(memory_space=pltpu.VMEM)
    sq = lambda t: pltpu.VMEM((side, side), t)
    wide = lambda t: pltpu.VMEM((2, side, third), t)
    return pl.pallas_call(
        functools.partial(solve_kernel, n_row),
        in_specs=[any_] * (2 * n_row),
        out_specs=[vm] * 3,
        out_shape=[
            jax.ShapeDtypeStruct((2, rows, third), F32),
            jax.ShapeDtypeStruct((2, side, third), BF16),
            jax.ShapeDtypeStruct((2, side, third), BF16),
        ],
        scratch_shapes=[
            sq(F32), sq(BF16), sq(BF16), sq(F32), sq(BF16), sq(BF16), sq(BF16), sq(BF16),
            wide(F32), wide(BF16), wide(BF16), wide(F32),
            pltpu.SemaphoreType.DMA((3, n_row)),
        ],
        compiler_params=pltpu.CompilerParams(vmem_limit_bytes=VMEM_LIMIT),
        cost_estimate=pl.CostEstimate(flops=3 * 2 * side * side * (2 * side + 2 * third), transcendentals=0, bytes_accessed=4 * side * (side + 4 * third)),
        name="solve_columns",
    )(*joints, *couplings)


def lift_kernel(slots, n_col, has_ee, *refs):
    blocks = refs[: len(slots)]
    base, head, tail, out = refs[len(slots) :]
    me = lax.axis_index("col")
    depth = head.shape[1] // n_col
    a = pl.program_id(0)
    parts = [split(block[0]) for block in blocks]
    for b in range(2):
        if has_ee:
            total = jnp.where(a == b, base[0], 0.0)
        else:
            total = base[0, b]
        for part, k in zip(parts, slots):
            at = pl.ds(pl.multiple_of(owner(me, k, n_col) * depth, depth), depth)
            total = total + dot3(part, (head[b, at], tail[b, at]))
        out[0, b] = total


def lift(blocks, slots, base, head, tail, n_col, has_ee):
    ext, depth = blocks[0].shape[1:]
    side, third = head.shape[1:]
    rt = tile_of(ext, 192)
    block = pl.BlockSpec((1, rt, depth), lambda a, t: (a, t, 0))
    result = pl.BlockSpec((1, 2, rt, third), lambda a, t: (a, 0, t, 0))
    sol = pl.BlockSpec((2, side, third), lambda a, t: (0, 0, 0))
    first = pl.BlockSpec((1, rt, third), lambda a, t: (a, t, 0)) if has_ee else result
    return pl.pallas_call(
        functools.partial(lift_kernel, slots, n_col, has_ee),
        grid=(2, ext // rt),
        in_specs=[block] * len(blocks) + [first, sol, sol],
        out_specs=result,
        out_shape=jax.ShapeDtypeStruct((2, 2, ext, third), F32),
        input_output_aliases={} if has_ee else {len(blocks): 0},
        compiler_params=pltpu.CompilerParams(vmem_limit_bytes=VMEM_LIMIT),
        cost_estimate=pl.CostEstimate(flops=3 * 8 * len(blocks) * ext * depth * third, transcendentals=0, bytes_accessed=4 * 6 * ext * third),
        name="lift_ee" if has_ee else "lift_add",
    )(*blocks, base, head, tail)


def boundary_rows(data, third):
    n_row, n_col = lax.axis_size("row"), lax.axis_size("col")
    if n_row == n_col:
        pairs = [(i * n_col + j, j * n_col + i) for i in range(n_row) for j in range(n_col)]
        turned = lax.ppermute(data, ("row", "col"), pairs)
        me = lax.axis_index("row")
        place = (lambda j: me ^ j) if pow2(n_row) else (lambda j: lax.rem(j - me + n_row, n_row))
        return jnp.stack(gather_slots(turned, "row")), place
    whole = lax.all_gather(data, "row", axis=1, tiled=True)
    rows = [lax.dynamic_slice_in_dim(whole, j * third, third, 1) for j in range(n_col)]
    swapped = lax.all_to_all(jnp.stack(rows), "col", split_axis=0, concat_axis=0, tiled=True)
    return swapped, lambda j: j


def shards(
    ext_ext,
    ext_int,
    int_ext,
    int_int,
    boundary_data,
    leaf_ext_ext,
    leaf_ext_int,
    leaf_int_ext,
    leaf_int_int,
):
    n_col = lax.axis_size("col")
    col = lax.axis_index("col")
    third = ext_ext.shape[2]
    joint = int_int[0] + int_int[1]
    joint_rows = jnp.concatenate(in_order(gather_slots(joint, "col"), "col"), axis=1)
    joints = gather_slots(joint_rows, "row")
    couplings = gather_slots(int_ext, "row")
    blocks = gather_slots(ext_int, "col")
    data, place = boundary_rows(boundary_data, third)

    leaf_parent, leaf_solve = leaf_merge(leaf_ext_ext, leaf_ext_int, leaf_int_ext, leaf_int_int)
    solve_op, head, tail = solve_columns(joints, couplings)

    early = list(range(n_col - 1))
    parent = lift(blocks[:-1], early, ext_ext, head, tail, n_col, True)
    parent_map = lift(blocks[-1:], [n_col - 1], parent, head, tail, n_col, False)

    parts = jnp.einsum("bnk,pbkq->pnq", solve_op, data, precision=lax.Precision.HIGHEST)
    pick = lambda j: lax.dynamic_index_in_dim(parts, place(j), 0, False)
    interface_values = pick(col)
    for k in range(1, n_col):
        target = owner(col, k, n_col) if pow2(n_col) else lax.rem(col - k + n_col, n_col)
        interface_values = interface_values + send(pick(target), "col", k)
    return (parent_map, solve_op, interface_values, leaf_parent, leaf_solve)


def solution(mesh):
    in_specs = (
        P("dom", "row", "col"),
        P("dom", "row", "col"),
        P("dom", "row", "col"),
        P("dom", "row", "col"),
        P("dom", "row", "col"),
        P(("dom", "row", "col"), None, None, None),
        P(("dom", "row", "col"), None, None, None),
        P(("dom", "row", "col"), None, None, None),
        P(("dom", "row", "col"), None, None, None),
    )
    out_specs = (
        P("dom", None, "row", "col"),
        P("dom", "row", "col"),
        P(("dom", "row"), "col"),
        P(("dom", "row", "col"), None, None, None, None),
        P(("dom", "row", "col"), None, None, None),
    )
    return jax.shard_map(shards, mesh=mesh, in_specs=in_specs, out_specs=out_specs, check_vma=False)
```
